256 devices in a mesh: pts: 32 (over x, y, z_lo), grid: 8 (over z_hi, core).
Axes of the slice: x: 4, y: 4, z: 8 (z_hi: 4, z_lo: 2; z = z_hi * 2 + z_lo), core: 2. Of those that a mesh axis runs over, the one named last changes fastest.
Arguments:
- probes: bfloat16 [8, 1024, 8, 128], P('grid', 'pts'), may hold values from -6 to 6
- weights: bfloat16 [8, 1024, 64, 128], P('grid', 'pts'), may hold values from -0.049804688 to 0.25
- brick_owner: int32 [8, 1024, 1], P('grid', 'pts'), may hold values from 0 to 31; in each aligned block of 32 rows (0 to 31, 32 to 63, ..., all dimensions but the last counted through in order) at most 2 rows name the same one
- brick_slot: int32 [8, 1024], P('grid', 'pts'), may hold values from 0 to 127
- counts: int32 [8, 1024], P('grid', 'pts'), may hold values from 64 to 128
- length_scale: float32 [1], replicated, may hold values from 0.015 to 0.05
Outputs:
- covariance_product: float32 [8, 1024, 8, 128], P('grid', 'pts')
- lengthscale_adjoint: float32 [8, 1024, 8, 128], P('grid', 'pts')
The draws below stay inside these ranges and needn't reach their ends.
Inputs may be any that keep to these rules, and one draw needn't show every extreme that they name: `brick_owner`: among the 32 blocks of one device, at most 2 have one owner, and some owner has exactly 2 of them.
All inputs are finite; a program needn't handle non-finite values.
Results may differ from the reference program's by a relative error of at most 0.0028.
Values may be sent and summed in bfloat16 or wider, within the bound.
A program may use at most 64 MiB of HBM per device.

```python
import math
import jax
import jax.numpy as jnp
import numpy as np
from jax import lax

GX = 128
GY = 128
GZ = 128
P_SIZE = 8
B = 128
NBLK = 32
XS = 16
BRICKS = 4096
BR_DEV = 128
CAP = 2
BLOCKS = 1024
N_PTS = 32
N_GRID = 8


def touch_ends(result, rng, low, high):
    spot = [jax.random.randint(jax.random.fold_in(rng, axis), (), 0, length) for axis, length in enumerate(result.shape)]
    widest = result.shape.index(max(result.shape))
    next_to = spot[:widest] + [(spot[widest] + 1) % result.shape[widest]] + spot[widest + 1:]
    return result.at[tuple(spot)].set(low).at[tuple(next_to)].set(high)


def levels(rng, dims, shards, low, largest):
    def one(dim, shards_of):
        steps = jax.random.uniform(jax.random.fold_in(jax.random.fold_in(rng, 6), dim), (shards_of,), jnp.float32, low / len(shards), largest / len(shards))
        return jnp.repeat(jnp.exp(steps), dims[dim] // shards_of).reshape((-1,) + (1,) * (len(dims) - dim - 1))

    level = one(*shards[0])
    for cut in shards[1:]:
        level = level * one(*cut)
    return level


def deal_out(stream_key, own, number, rows, amount, top, limit, skew):
    sequence = jax.random.permutation(stream_key, amount)
    packed, common = load_shares(amount, rows * top, limit, skew, True), load_shares(amount, rows * top, limit, skew, False)
    places = jnp.arange(amount)

    def named(tallies, offset_by):
        used = int((tallies > 0).sum())
        fixed = max(1, used // 4)
        passed = fixed + (places - fixed + offset_by * (used - fixed)) % max(1, amount - fixed)
        return jnp.zeros((amount,), jnp.int32).at[sequence[jnp.where(places < fixed, places, passed)]].set(jnp.asarray(tallies, jnp.int32))

    tallies = jnp.where(number % 4 == 0, named(packed, number // 4), named(common, number - number // 4 - 1))
    mixed = jax.random.permutation(jax.random.fold_in(own, 3), amount)
    source_of, taker = mixed[0:amount // 2 * 2:2], mixed[1:amount // 2 * 2:2]
    slack = jnp.minimum(tallies[source_of] - 1, limit - tallies[taker]) // 2
    slack = jnp.where((source_of == sequence[0]) | (taker == sequence[0]) | (tallies[taker] == 0), 0, jnp.maximum(slack, 0))
    passed = jax.random.randint(jax.random.fold_in(own, 4), (amount // 2,), 0, 1 << 20) % (slack + 1)
    tallies = tallies.at[source_of].add(-passed).at[taker].add(passed)
    labels = jnp.searchsorted(jnp.cumsum(tallies), jnp.arange(rows * top), side="right").astype(jnp.int32)
    table = labels.reshape(top, rows).T
    table = table[jax.random.permutation(jax.random.fold_in(own, 1), rows)]
    offset_by = jax.random.randint(jax.random.fold_in(own, 2), (rows, 1), 0, top)
    return jnp.take_along_axis(table, (jnp.arange(top)[None, :] + offset_by) % top, axis=1)


def load_shares(count, total, reach, lean, full):
    loads = [(1 << 20) // math.isqrt(grade ** lean) + 1 for grade in range(1, count + 1)]
    largest = reach if full else min(reach, max(-(-total // count), total * loads[0] // sum(loads)))
    least = 1 if total - largest >= count - 1 else 0
    given, rest = [largest] + [least] * (count - 1), total - largest - least * (count - 1)
    while rest > 0:
        movable = [i for i in range(1, count) if given[i] < largest] or [i for i in range(1, count) if given[i] < reach]
        pool, left = sum([loads[i] for i in movable]), rest
        for i in movable:
            addition = min(reach - given[i], max(1, left * loads[i] // pool), rest)
            given[i] = given[i] + addition
            rest = rest - addition
    return np.array(given)


def scatter_about(own_key, shape, scale, most, cuts=(), held_as=jnp.bfloat16):
    gain = levels(own_key, shape, cuts, -0.22, 0.18) if cuts else 1.0
    values = jax.random.normal(own_key, shape, jnp.float32) * scale * gain
    return jnp.minimum(jnp.maximum(values, -most), most).astype(held_as)


def setup_inputs(seed: int = 0) -> dict:
    keys = jax.random.split(jax.random.key(seed), 7)
    probes = scatter_about(keys[0], (N_GRID, BLOCKS, P_SIZE, B), 1.0, 6.0, ((0, 8), (1, 32)))
    weights = jnp.clip(-0.049804688 + 0.2998047 * jax.random.uniform(keys[1], (N_GRID, BLOCKS, 64, B), jnp.float32) ** levels(keys[1], (N_GRID, BLOCKS, 64, B), ((0, 8), (1, 32)), -0.2, 0.2), -0.049804688, 0.25).astype(jnp.bfloat16)
    brick_owner_keys = jax.random.split(jax.random.fold_in(keys[2], 1), N_GRID * BLOCKS // NBLK)
    brick_owner_turns = jax.random.permutation(jax.random.fold_in(keys[2], 3), N_GRID * BLOCKS // NBLK)
    brick_owner = jax.vmap(lambda own, number: deal_out(jax.random.fold_in(keys[2], 2), own, number, NBLK, N_PTS, 1, CAP, 1))(brick_owner_keys, brick_owner_turns).reshape((N_GRID, BLOCKS, 1))
    brick_slot = touch_ends(jax.random.randint(keys[3], (N_GRID, BLOCKS), 0, BR_DEV), jax.random.fold_in(keys[3], 1), 0, BR_DEV - 1).astype(jnp.int32)
    counts = touch_ends(jax.random.randint(keys[4], (N_GRID, BLOCKS), B // 2, B + 1), jax.random.fold_in(keys[4], 1), B // 2, B).astype(jnp.int32)
    length_scale = jnp.clip(jnp.exp(jax.random.uniform(keys[5], (1,), jnp.float32, math.log(0.015), math.log(0.05))), 0.015, 0.05)
    return dict(probes=probes, weights=weights, brick_owner=brick_owner, brick_slot=brick_slot, counts=counts, length_scale=length_scale)


ROOT_FIVE = math.sqrt(5.0)

def matern_tables(length_scale, extent):
    ell = length_scale[0]
    places = jnp.arange(extent).astype(jnp.float32)
    spread = jnp.abs(places[:, None] - places[None, :]) / extent
    scaled = ROOT_FIVE * spread / ell
    decay = jnp.exp(-scaled)
    factor = 1.0 / jnp.sqrt(extent * ell)
    poly = 1.0 + scaled + scaled * scaled / 3.0
    value = poly * decay * factor
    slope = (scaled * scaled * (1.0 + scaled) / 3.0 - 0.5 * poly) * decay * factor
    return (value, slope)

def reference(probes, weights, brick_owner, brick_slot, counts, length_scale):
    precise = lax.Precision.HIGHEST
    span_x = XS // 4
    span_y = GY // 4
    span_z = GZ // 4

    def usable_of(count_row):
        return (jnp.arange(B).astype(jnp.int32)[None, :] < count_row[:, None]).astype(jnp.float32)

    def slab_partial(inputs):
        weight_slab, probe_slab, owner_slab, slot_slab, count_slab = inputs
        usable = usable_of(count_slab)
        masked = probe_slab * usable[:, None, :].astype(probe_slab.dtype)
        bricks = owner_slab[:, 0] * BR_DEV + slot_slab
        sums = jnp.einsum('bcn,bpn->bpc', weight_slab.astype(jnp.float32), masked.astype(jnp.float32))
        return jnp.zeros((BRICKS, P_SIZE, 64), jnp.float32).at[bricks].add(sums)
    brick_fields = lax.map(slab_partial, (weights, probes, brick_owner, brick_slot, counts))
    shaped = brick_fields.reshape(N_GRID, span_x, span_y, span_z, P_SIZE, 4, 4, 4)
    field = shaped.transpose(4, 0, 1, 5, 2, 6, 3, 7).reshape(P_SIZE, GX, GY, GZ)
    kx_value, kx_slope = matern_tables(length_scale, GX)
    ky_value, ky_slope = matern_tables(length_scale, GY)
    kz_value, kz_slope = matern_tables(length_scale, GZ)

    def apply_factors(single):
        along_z = jnp.einsum('xyz,kz->xyk', single, kz_value, precision=precise)
        slope_z = jnp.einsum('xyz,kz->xyk', single, kz_slope, precision=precise)
        both_y = jnp.einsum('xyz,wy->xwz', along_z, ky_value, precision=precise)
        slope_y = jnp.einsum('xyz,wy->xwz', along_z, ky_slope, precision=precise)
        cross_y = jnp.einsum('xyz,wy->xwz', slope_z, ky_value, precision=precise)
        value = jnp.einsum('xyz,vx->vyz', both_y, kx_value, precision=precise)
        slope = jnp.einsum('xyz,vx->vyz', both_y, kx_slope, precision=precise)
        slope = slope + jnp.einsum('xyz,vx->vyz', slope_y + cross_y, kx_value, precision=precise)
        return (value.astype(jnp.bfloat16), slope.astype(jnp.bfloat16))
    grid_value, grid_slope = lax.map(apply_factors, field)

    def to_bricks(grid_field):
        parted = grid_field.reshape(P_SIZE, N_GRID, span_x, 4, span_y, 4, span_z, 4)
        return parted.transpose(1, 2, 4, 6, 0, 3, 5, 7).reshape(N_GRID, BRICKS, P_SIZE, 64)
    value_bricks = to_bricks(grid_value)
    slope_bricks = to_bricks(grid_slope)

    def slab_output(inputs):
        weight_slab, owner_slab, slot_slab, count_slab, value_slab, slope_slab = inputs
        usable = usable_of(count_slab)
        bricks = owner_slab[:, 0] * BR_DEV + slot_slab
        value_rows = jnp.take(value_slab, bricks, axis=0).astype(jnp.float32)
        slope_rows = jnp.take(slope_slab, bricks, axis=0).astype(jnp.float32)
        weight_wide = weight_slab.astype(jnp.float32)
        product = jnp.einsum('bcn,bpc->bpn', weight_wide, value_rows) * usable[:, None, :]
        adjoint = jnp.einsum('bcn,bpc->bpn', weight_wide, slope_rows) * usable[:, None, :]
        return (product, adjoint)
    covariance_product, lengthscale_adjoint = lax.map(slab_output, (weights, brick_owner, brick_slot, counts, value_bricks, slope_bricks))
    return (covariance_product, lengthscale_adjoint)
```

```python
import math

import jax
import jax.numpy as jnp
from jax import lax
from jax.experimental import pallas as pl
from jax.experimental.pallas import tpu as pltpu
from jax.sharding import PartitionSpec as P

EXTENT = 128
ROOT_FIVE = math.sqrt(5.0)
F32 = jnp.float32
BF16 = jnp.bfloat16
I32 = jnp.int32
PEERS = 32


def iota(shape, dim):
    return lax.broadcasted_iota(I32, shape, dim)


def matern(distance, ell):
    scaled = (ROOT_FIVE / EXTENT) * distance / ell
    scale = jnp.exp(-scaled) * lax.rsqrt(EXTENT * ell)
    poly = 1.0 + scaled + scaled * scaled * (1.0 / 3.0)
    value = poly * scale
    slope = (scaled * scaled * (1.0 + scaled) * (1.0 / 3.0) - 0.5 * poly) * scale
    return value, slope


def split(table):
    high = table.astype(BF16)
    low = (table - high.astype(F32)).astype(BF16)
    return high, low


def swapped(place):
    return 4 * (place % 32) + place // 32


def dot(a, b):
    return jnp.dot(a, b, preferred_element_type=F32)


def kernel(
    owner_ref, slot_ref, count_ref, scale_ref, probe_ref, weight_ref, cov_ref, adj_ref,
    sums, sel, lines, field, pieces,
    send1, recv1, send2, recv2, send3, recv3, send4, recv4,
    send_sem, recv_sem,
):
    g = lax.axis_index("grid")
    i = lax.axis_index("pts")
    probe = i // 4
    mine = g * 4 + i % 4

    def pts_peer(k):
        return g, k

    def line_peer(k):
        return k // 4, probe * 4 + k % 4

    barrier = pltpu.get_barrier_semaphore()

    def greet(step, carry):
        for me, peer in ((i, pts_peer), (mine, line_peer)):
            to_g, to_i = peer(lax.rem(me + step, PEERS))
            pl.semaphore_signal(
                barrier, inc=1, device_id={"grid": to_g, "pts": to_i}, device_id_type=pl.DeviceIdType.MESH
            )
        return carry

    lax.fori_loop(1, PEERS, greet, 0)

    def copy(phase, me, peer, source, target, k):
        to_g, to_i = peer(k)
        return pltpu.make_async_remote_copy(
            src_ref=source.at[k],
            dst_ref=target.at[me],
            send_sem=send_sem.at[phase],
            recv_sem=recv_sem.at[phase],
            device_id={"grid": to_g, "pts": to_i},
            device_id_type=pl.DeviceIdType.MESH,
        )

    def start(phase, me, peer, source, target):
        def one(step, carry):
            copy(phase, me, peer, source, target, lax.rem(me + step, PEERS)).start()
            return carry

        lax.fori_loop(1, PEERS, one, 0)
        target[me] = source[me]

    def finish(phase, source, target):
        whole = pltpu.make_async_remote_copy(
            src_ref=source.at[pl.ds(0, PEERS - 1)],
            dst_ref=target.at[pl.ds(0, PEERS - 1)],
            send_sem=send_sem.at[phase],
            recv_sem=recv_sem.at[phase],
            device_id={"grid": g, "pts": i},
            device_id_type=pl.DeviceIdType.MESH,
        )
        whole.wait_send()
        whole.wait_recv()

    ell = jnp.full((1, 1), scale_ref[0], F32)
    lane8 = iota((8, 128), 1)

    used = [jnp.int32(0)] * 4
    lane512 = iota((8, 512), 1)
    probe_row = iota((8, 512), 0) == lane512 // 64
    blocks = probe_ref.shape[0]
    for b in range(blocks):
        owner = owner_ref[0, b]
        slot = slot_ref[0, b]
        column = owner // 8
        rank = jnp.int32(0)
        for c in range(4):
            here = column == c
            rank = jnp.where(here, used[c], rank)
            used[c] = used[c] + here.astype(I32)
        place = column * 16 + rank
        brick_y = (owner % 8) * 4 + slot // 32
        brick_z = slot % 32
        masked = jnp.where(lane8 < count_ref[0, b], probe_ref[b].astype(F32), 0.0).astype(BF16)
        padded = jnp.concatenate([weight_ref[b], jnp.zeros((64, 128), BF16)], axis=0)
        block_sum = lax.dot_general(masked, padded, (((1,), (1,)), ((), ())), preferred_element_type=F32)
        block_sum = jnp.where(lane8 == 64, brick_y.astype(F32), block_sum)
        block_sum = jnp.where(lane8 == 65, brick_z.astype(F32), block_sum)
        sums[pl.ds(b * 8, 8), :] = block_sum
        chosen = probe_row & (lane512 % 64 == place)
        sel[pl.ds(b * 8, 8), :] = chosen.astype(F32)

    spread = sel[...].T.astype(BF16)
    message = dot(spread, sums[...].astype(BF16))
    send1[...] = message.astype(BF16).reshape(PEERS, 16, 128)

    pl.semaphore_wait(barrier, 2 * (PEERS - 1))
    start(0, i, pts_peer, send1, recv1)

    row_z, lane_z = iota((128, 256), 0), iota((128, 256), 1)
    value, slope = matern(jnp.abs(swapped(row_z) - swapped(lane_z % 128)).astype(F32), ell)
    along_z = jnp.concatenate(split(jnp.where(lane_z < 128, value, slope)), axis=0)
    row_y, lane_y = iota((256, 128), 0), iota((256, 128), 1)
    value, slope = matern(jnp.abs(swapped(row_y % 128) - swapped(lane_y)).astype(F32), ell)
    along_y = jnp.concatenate(split(jnp.where(row_y < 128, value, slope)), axis=1)
    row_x, lane_x = iota((256, 256), 0), iota((256, 256), 1)
    x_out = (row_x // 8) * 4 + row_x % 4
    x_in = (lane_x // 8) * 4 + lane_x % 4
    value, slope = matern(jnp.abs(x_out - x_in).astype(F32), ell)
    out_slope = (row_x // 4) % 2
    in_mixed = (lane_x // 4) % 2
    table_x = jnp.where(out_slope == in_mixed, value, jnp.where(out_slope == 1, slope, 0.0))
    along_x = jnp.concatenate(split(table_x), axis=1)

    finish(0, send1, recv1)

    arrived = recv1[...].reshape(PEERS * 16, 128)
    wide = arrived.astype(F32)
    at_y = wide[:, 64:65].astype(I32)
    at_z = wide[:, 65:66].astype(I32)
    lane_s = iota((PEERS * 16, 128), 1)
    is_z = at_z == lane_s % 32
    is_y = (at_y == lane_s).astype(F32)
    is_y_across = is_y.T[0:32].astype(BF16)
    is_y = is_y.astype(BF16)
    cell = iota((128, 256), 0)
    lane = iota((128, 256), 1)
    is_z2 = jnp.concatenate([is_z, is_z], axis=1)
    for t in range(8):
        copies = (cell == t * 8 + lane // 32).astype(F32).astype(BF16)
        placed = jnp.where(is_z2, dot(arrived, copies), 0.0).astype(BF16)
        rows = dot(is_y_across, placed)
        lines[pl.ds(t * 64, 32), :] = rows[:, 0:128]
        lines[pl.ds(t * 64 + 32, 32), :] = rows[:, 128:256]

    cells = lines[...].astype(BF16)
    by_z = dot(jnp.concatenate([cells, cells], axis=1), along_z).astype(BF16)
    for cx in range(4):
        part = by_z[cx * 128 : (cx + 1) * 128]
        by_y = dot(along_y, jnp.concatenate([part, part], axis=0))
        field[pl.ds(cx, 128, stride=8), :] = by_y[0:128, 0:128]
        field[pl.ds(4 + cx, 128, stride=8), :] = by_y[0:128, 128:256] + by_y[128:256, 0:128]
    send2[...] = field[...].astype(BF16).reshape(PEERS, 32, 128)
    start(1, mine, line_peer, send2, recv2)
    finish(1, send2, recv2)

    got = recv2[...].astype(F32)
    for j in range(4):
        part = got[:, j * 8 : (j + 1) * 8, :].reshape(256, 128).astype(BF16)
        by_x = dot(along_x, jnp.concatenate([part, part], axis=0))
        pieces[:, j * 8 : (j + 1) * 8, :] = by_x.reshape(PEERS, 8, 128)
    send3[...] = pieces[...].astype(BF16)
    start(2, mine, line_peer, send3, recv3)
    finish(2, send3, recv3)

    field[...] = recv3[...].astype(F32).reshape(1024, 128)
    is_y32 = is_y[:, 0:32]
    total = jnp.zeros((PEERS * 16, 128), F32)
    row2, lane2 = iota((256, 128), 0), iota((256, 128), 1)
    for t in range(16):
        pair = []
        for u in (2 * t, 2 * t + 1):
            which, cy = u // 4, u % 4
            pair.append(field[pl.ds(cy * 256 + which, 32, stride=8), :])
        rows = jnp.concatenate(pair, axis=1).astype(BF16)
        taken = jnp.where(is_z2, dot(is_y32, rows), 0.0).astype(BF16)
        gather = (lane2 == t * 8 + row2 // 32).astype(F32).astype(BF16)
        total = total + dot(taken, gather)
    send4[...] = total.astype(BF16).reshape(PEERS, 16, 128)
    start(3, i, pts_peer, send4, recv4)
    finish(3, send4, recv4)

    sums[...] = dot(sel[...].astype(BF16), recv4[...].reshape(PEERS * 16, 128))
    for b in range(blocks):
        block = sums[pl.ds(b * 8, 8), :]
        both = jnp.concatenate([jnp.where(lane8 < 64, block, 0.0), jnp.where(lane8 < 64, 0.0, block)], axis=0)
        twice = jnp.concatenate([weight_ref[b], weight_ref[b]], axis=0)
        result = dot(both.astype(BF16), twice)
        usable = lane8 < count_ref[0, b]
        cov_ref[b] = jnp.where(usable, result[0:8], 0.0)
        adj_ref[b] = jnp.where(usable, result[8:16], 0.0)


def on_device(probes, weights, brick_owner, brick_slot, counts, length_scale):
    blocks = probes.shape[1]
    smem = pl.BlockSpec(memory_space=pltpu.SMEM)
    vmem = pl.BlockSpec(memory_space=pltpu.VMEM)
    out = jax.ShapeDtypeStruct((blocks, 8, 128), F32)
    small = pltpu.VMEM((PEERS, 16, 128), BF16)
    large = pltpu.VMEM((PEERS, 32, 128), BF16)
    cov, adj = pl.pallas_call(
        kernel,
        out_shape=(out, out),
        in_specs=[smem, smem, smem, smem, vmem, vmem],
        out_specs=(vmem, vmem),
        scratch_shapes=[
            pltpu.VMEM((256, 128), F32),
            pltpu.VMEM((256, 512), F32),
            pltpu.VMEM((512, 128), F32),
            pltpu.VMEM((1024, 128), F32),
            pltpu.VMEM((PEERS, 32, 128), F32),
            small, small, large, large, large, large, small, small,
            pltpu.SemaphoreType.DMA((4,)),
            pltpu.SemaphoreType.DMA((4,)),
        ],
        compiler_params=pltpu.CompilerParams(collective_id=0, has_side_effects=True),
        name="covariance",
    )(brick_owner.reshape(1, blocks), brick_slot, counts, length_scale, probes[0], weights[0])
    return cov[None], adj[None]


def solution(mesh):
    placed = (
        P("grid", "pts", None, None),
        P("grid", "pts", None, None),
        P("grid", "pts", None),
        P("grid", "pts"),
        P("grid", "pts"),
        P(),
    )
    return jax.shard_map(
        on_device,
        mesh=mesh,
        in_specs=placed,
        out_specs=(P("grid", "pts", None, None), P("grid", "pts", None, None)),
        check_vma=False,
    )
```

```python
import functools
import math

import jax
import jax.numpy as jnp
from jax import lax
from jax.experimental import pallas as pl
from jax.experimental.pallas import tpu as pltpu
from jax.sharding import PartitionSpec as P

EXTENT = 128
ROOT_FIVE = math.sqrt(5.0)
F32 = jnp.float32
BF16 = jnp.bfloat16
I32 = jnp.int32
PEERS = 32


def iota(shape, dim):
    return lax.broadcasted_iota(I32, shape, dim)


def matern(distance, ell):
    scaled = (ROOT_FIVE / EXTENT) * distance / ell
    scale = jnp.exp(-scaled) * lax.rsqrt(EXTENT * ell)
    poly = 1.0 + scaled + scaled * scaled * (1.0 / 3.0)
    value = poly * scale
    slope = (scaled * scaled * (1.0 + scaled) * (1.0 / 3.0) - 0.5 * poly) * scale
    return value, slope


def split(table):
    high = table.astype(BF16)
    low = (table - high.astype(F32)).astype(BF16)
    return high, low


def swapped(place):
    return 4 * (place % 32) + place // 32


def dot(a, b):
    return jnp.dot(a, b, preferred_element_type=F32)


def kernel(
    chunks, owner_ref, slot_ref, count_ref, scale_ref, probe_ref, weight_ref, rows_ref,
    sums, sel, lines, field, total,
    send1, recv1, send2, recv2, send3, recv3, send4, recv4,
    send_sem, recv_sem,
):
    g = lax.axis_index("grid")
    i = lax.axis_index("pts")
    probe = i // 4
    mine = g * 4 + i % 4
    at_z, core = (g // 2) * 2 + i % 2, g % 2
    per = 4 // chunks

    def hops(shift, size):
        return min(shift, size - shift)

    def farthest(sizes):
        shifts = [()]
        for size in sizes:
            shifts = [old + (new,) for old in shifts for new in range(size)]
        return shifts

    pts_shifts = sorted(farthest((4, 4, 2))[1:], key=lambda s: -hops(s[0], 4) - hops(s[1], 4) - s[2])
    line_shifts = sorted(farthest((8, 2, 2))[1:], key=lambda s: -hops(s[0], 8) - s[1] - 0.1 * s[2])

    def pts_peer(shift):
        to = lax.rem(i // 8 + shift[0], 4) * 8 + lax.rem(i // 2 % 4 + shift[1], 4) * 2 + lax.rem(i % 2 + shift[2], 2)
        return to, {"grid": g, "pts": to}

    def line_peer(shift):
        z = lax.rem(at_z + shift[0], 8)
        place = lax.rem(i // 2 % 2 + shift[1], 2) * 2 + z % 2
        to_g = (z // 2) * 2 + lax.rem(core + shift[2], 2)
        return to_g * 4 + place, {"grid": to_g, "pts": probe * 4 + place}

    barrier = pltpu.get_barrier_semaphore()
    for peer, shifts in ((line_peer, line_shifts), (pts_peer, pts_shifts)):
        for shift in shifts:
            pl.semaphore_signal(barrier, inc=1, device_id=peer(shift)[1], device_id_type=pl.DeviceIdType.MESH)

    def start(sem, me, peer, shifts, source, target):
        for shift in shifts:
            k, device = peer(shift)
            pltpu.make_async_remote_copy(
                src_ref=source.at[k],
                dst_ref=target.at[me],
                send_sem=send_sem.at[sem],
                recv_sem=recv_sem.at[sem],
                device_id=device,
                device_id_type=pl.DeviceIdType.MESH,
            ).start()
        target[me] = source[me]

    def whole(sem, source, target):
        return pltpu.make_async_remote_copy(
            src_ref=source.at[pl.ds(0, PEERS - 1)],
            dst_ref=target.at[pl.ds(0, PEERS - 1)],
            send_sem=send_sem.at[sem],
            recv_sem=recv_sem.at[sem],
            device_id={"grid": g, "pts": i},
            device_id_type=pl.DeviceIdType.MESH,
        )

    ell = jnp.full((1, 1), scale_ref[0], F32)
    lane8 = iota((8, 128), 1)

    used = [jnp.int32(0)] * 4
    lane512 = iota((8, 512), 1)
    probe_row = iota((8, 512), 0) == lane512 // 64
    blocks = probe_ref.shape[0]
    for b in range(blocks):
        owner = owner_ref[0, b]
        slot = slot_ref[0, b]
        column = owner // 8
        rank = jnp.int32(0)
        for c in range(4):
            here = column == c
            rank = jnp.where(here, used[c], rank)
            used[c] = used[c] + here.astype(I32)
        place = column * 16 + rank
        brick_y = (owner % 8) * 4 + slot // 32
        brick_z = slot % 32
        masked = jnp.where(lane8 < count_ref[0, b], probe_ref[b].astype(F32), 0.0).astype(BF16)
        padded = jnp.concatenate([weight_ref[b], jnp.zeros((64, 128), BF16)], axis=0)
        block_sum = lax.dot_general(masked, padded, (((1,), (1,)), ((), ())), preferred_element_type=F32)
        block_sum = jnp.where(lane8 == 64, brick_y.astype(F32), block_sum)
        block_sum = jnp.where(lane8 == 65, brick_z.astype(F32), block_sum)
        sums[pl.ds(b * 8, 8), :] = block_sum
        chosen = probe_row & (lane512 % 64 == place)
        sel[pl.ds(b * 8, 8), :] = chosen.astype(F32)

    spread = sel[...].T.astype(BF16)
    message = dot(spread, sums[...].astype(BF16))
    send1[...] = message.astype(BF16).reshape(PEERS, 16, 128)

    pl.semaphore_wait(barrier, 2 * (PEERS - 1))
    start(0, i, pts_peer, pts_shifts, send1, recv1)

    row_z, lane_z = iota((128, 256), 0), iota((128, 256), 1)
    value, slope = matern(jnp.abs(swapped(row_z) - swapped(lane_z % 128)).astype(F32), ell)
    along_z = jnp.concatenate(split(jnp.where(lane_z < 128, value, slope)), axis=0)
    row_y, lane_y = iota((256, 128), 0), iota((256, 128), 1)
    value, slope = matern(jnp.abs(swapped(row_y % 128) - swapped(lane_y)).astype(F32), ell)
    along_y = jnp.concatenate(split(jnp.where(row_y < 128, value, slope)), axis=1)
    row_x, lane_x = iota((256, 256), 0), iota((256, 256), 1)
    x_out = (row_x // 8) * 4 + row_x % 4
    x_in = (lane_x // 8) * 4 + lane_x % 4
    value, slope = matern(jnp.abs(x_out - x_in).astype(F32), ell)
    out_slope = (row_x // 4) % 2
    in_mixed = (lane_x // 4) % 2
    table_x = jnp.where(out_slope == in_mixed, value, jnp.where(out_slope == 1, slope, 0.0))
    along_x = jnp.concatenate(split(table_x), axis=1)

    whole(0, send1, recv1).wait_recv()

    arrived = recv1[...].reshape(PEERS * 16, 128)
    wide = arrived.astype(F32)
    brick_y = wide[:, 64:65].astype(I32)
    brick_z = wide[:, 65:66].astype(I32)
    lane_s = iota((PEERS * 16, 128), 1)
    is_z = brick_z == lane_s % 32
    is_y = (brick_y == lane_s).astype(F32)
    is_y_across = is_y.T[0:32].astype(BF16)
    is_y = is_y.astype(BF16)
    cell = iota((128, 256), 0)
    lane = iota((128, 256), 1)
    is_z2 = jnp.concatenate([is_z, is_z], axis=1)
    for t in range(8):
        copies = (cell == t * 8 + lane // 32).astype(F32).astype(BF16)
        placed = jnp.where(is_z2, dot(arrived, copies), 0.0).astype(BF16)
        rows = dot(is_y_across, placed)
        lines[pl.ds(t * 64, 32), :] = rows[:, 0:128]
        lines[pl.ds(t * 64 + 32, 32), :] = rows[:, 128:256]

    cells = lines[...].astype(BF16)
    by_z = dot(jnp.concatenate([cells, cells], axis=1), along_z).astype(BF16)
    for cx in range(4):
        part = by_z[cx * 128 : (cx + 1) * 128]
        by_y = dot(along_y, jnp.concatenate([part, part], axis=0))
        field[pl.ds(cx, 128, stride=8), :] = by_y[0:128, 0:128]
        field[pl.ds(4 + cx, 128, stride=8), :] = by_y[0:128, 128:256] + by_y[128:256, 0:128]
    for c in range(chunks):
        for k in range(per):
            cy = c * per + k
            send2[c, :, k] = field[pl.ds(cy * 256, 256), :].reshape(PEERS, 8, 128).astype(BF16)
        start(1 + c, mine, line_peer, line_shifts, send2.at[c], recv2.at[c])

    for c in range(chunks):
        whole(1 + c, send2.at[c], recv2.at[c]).wait_recv()
        for k in range(per):
            part = recv2[c, :, k].astype(F32).reshape(256, 128).astype(BF16)
            by_x = dot(along_x, jnp.concatenate([part, part], axis=0))
            send3[c, :, k] = by_x.reshape(PEERS, 8, 128).astype(BF16)
        start(1 + chunks + c, mine, line_peer, line_shifts, send3.at[c], recv3.at[c])

    is_y32 = is_y[:, 0:32]
    row2, lane2 = iota((256, 128), 0), iota((256, 128), 1)
    for c in range(chunks):
        whole(1 + chunks + c, send3.at[c], recv3.at[c]).wait_recv()
        for k in range(per):
            cy = c * per + k
            field[pl.ds(cy * 256, 256), :] = recv3[c, :, k].astype(F32).reshape(256, 128)
            gathered = jnp.zeros((PEERS * 16, 128), F32)
            for w in (0, 2, 4, 6):
                pair = [field[pl.ds(cy * 256 + w + u, 32, stride=8), :] for u in range(2)]
                rows = jnp.concatenate(pair, axis=1).astype(BF16)
                taken = jnp.where(is_z2, dot(is_y32, rows), 0.0).astype(BF16)
                cell_of = (w + row2 // 128) * 16 + cy * 4 + row2 % 128 // 32
                gathered = gathered + dot(taken, (lane2 == cell_of).astype(F32).astype(BF16))
            if cy == 0:
                total[...] = gathered
            elif cy < 3:
                total[...] = total[...] + gathered
            else:
                send4[...] = (total[...] + gathered).astype(BF16).reshape(PEERS, 16, 128)
    last = 1 + 2 * chunks
    start(last, i, pts_peer, pts_shifts, send4, recv4)
    whole(0, send1, recv1).wait_send()
    for c in range(chunks):
        whole(1 + c, send2.at[c], recv2.at[c]).wait_send()
        whole(1 + chunks + c, send3.at[c], recv3.at[c]).wait_send()
    whole(last, send4, recv4).wait_recv()
    rows_ref[...] = dot(sel[...].astype(BF16), recv4[...].reshape(PEERS * 16, 128))
    whole(last, send4, recv4).wait_send()


def points_kernel(count_ref, rows_ref, weight_ref, cov_ref, adj_ref):
    lane8 = iota((8, 128), 1)
    for b in range(weight_ref.shape[0]):
        block = rows_ref[pl.ds(b * 8, 8), :]
        both = jnp.concatenate([jnp.where(lane8 < 64, block, 0.0), jnp.where(lane8 < 64, 0.0, block)], axis=0)
        twice = jnp.concatenate([weight_ref[b], weight_ref[b]], axis=0)
        result = dot(both.astype(BF16), twice)
        usable = lane8 < count_ref[0, b]
        cov_ref[b] = jnp.where(usable, result[0:8], 0.0)
        adj_ref[b] = jnp.where(usable, result[8:16], 0.0)


CHUNKS = 4


def on_device(probes, weights, brick_owner, brick_slot, counts, length_scale):
    blocks = probes.shape[1]
    chunks = CHUNKS
    smem = pl.BlockSpec(memory_space=pltpu.SMEM)
    vmem = pl.BlockSpec(memory_space=pltpu.VMEM)
    small = pltpu.VMEM((PEERS, 16, 128), BF16)
    large = pltpu.VMEM((chunks, PEERS, 4 // chunks, 8, 128), BF16)
    rows = pl.pallas_call(
        functools.partial(kernel, chunks),
        out_shape=jax.ShapeDtypeStruct((blocks * 8, 128), F32),
        in_specs=[smem, smem, smem, smem, vmem, vmem],
        out_specs=vmem,
        scratch_shapes=[
            pltpu.VMEM((256, 128), F32),
            pltpu.VMEM((256, 512), F32),
            pltpu.VMEM((512, 128), F32),
            pltpu.VMEM((1024, 128), F32),
            pltpu.VMEM((512, 128), F32),
            small, small, large, large, large, large, small, small,
            pltpu.SemaphoreType.DMA((2 + 2 * chunks,)),
            pltpu.SemaphoreType.DMA((2 + 2 * chunks,)),
        ],
        compiler_params=pltpu.CompilerParams(collective_id=0, has_side_effects=True),
        name="covariance",
    )(brick_owner.reshape(1, blocks), brick_slot, counts, length_scale, probes[0], weights[0])
    out = jax.ShapeDtypeStruct((blocks, 8, 128), F32)
    cov, adj = pl.pallas_call(
        points_kernel,
        out_shape=(out, out),
        in_specs=[smem, vmem, vmem],
        out_specs=(vmem, vmem),
        name="points",
    )(counts, rows, weights[0])
    return cov[None], adj[None]


def solution(mesh):
    placed = (
        P("grid", "pts", None, None),
        P("grid", "pts", None, None),
        P("grid", "pts", None),
        P("grid", "pts"),
        P("grid", "pts"),
        P(),
    )
    return jax.shard_map(
        on_device,
        mesh=mesh,
        in_specs=placed,
        out_specs=(P("grid", "pts", None, None), P("grid", "pts", None, None)),
        check_vma=False,
    )
```

```python
import functools
import math

import jax
import jax.numpy as jnp
from jax import lax
from jax.experimental import pallas as pl
from jax.experimental.pallas import tpu as pltpu
from jax.sharding import PartitionSpec as P

EXTENT = 128
ROOT_FIVE = math.sqrt(5.0)
F32 = jnp.float32
BF16 = jnp.bfloat16
I32 = jnp.int32
PEERS = 32


def iota(shape, dim):
    return lax.broadcasted_iota(I32, shape, dim)


def matern(distance, ell):
    scaled = (ROOT_FIVE / EXTENT) * distance / ell
    scale = jnp.exp(-scaled) * lax.rsqrt(EXTENT * ell)
    poly = 1.0 + scaled + scaled * scaled * (1.0 / 3.0)
    value = poly * scale
    slope = (scaled * scaled * (1.0 + scaled) * (1.0 / 3.0) - 0.5 * poly) * scale
    return value, slope


def split(table):
    high = table.astype(BF16)
    low = (table - high.astype(F32)).astype(BF16)
    return high, low


def swapped(place):
    return 4 * (place % 32) + place // 32


def dot(a, b):
    return jnp.dot(a, b, preferred_element_type=F32)


def kernel(
    chunks, owner_hbm, slot_hbm, count_hbm, probe_hbm, weight_hbm, scale_hbm, rows_ref,
    owner_ref, slot_ref, count_ref, scale_ref, probe_ref, weight_ref, sums, sel, lines, field, total,
    send1, recv1, send2, recv2, send3, recv3, send4, recv4,
    send_sem, recv_sem, load_sem,
):
    g = lax.axis_index("grid")
    i = lax.axis_index("pts")
    probe = i // 4
    mine = g * 4 + i % 4
    at_z, core = (g // 2) * 2 + i % 2, g % 2
    per = 4 // chunks

    def hops(shift, size):
        return min(shift, size - shift)

    def farthest(sizes):
        shifts = [()]
        for size in sizes:
            shifts = [old + (new,) for old in shifts for new in range(size)]
        return shifts

    pts_shifts = sorted(farthest((4, 4, 2))[1:], key=lambda s: -hops(s[0], 4) - hops(s[1], 4) - s[2])
    line_shifts = sorted(farthest((8, 2, 2))[1:], key=lambda s: -hops(s[0], 8) - s[1] - 0.1 * s[2])

    def pts_peer(shift):
        to = lax.rem(i // 8 + shift[0], 4) * 8 + lax.rem(i // 2 % 4 + shift[1], 4) * 2 + lax.rem(i % 2 + shift[2], 2)
        return to, {"grid": g, "pts": to}

    def line_peer(shift):
        z = lax.rem(at_z + shift[0], 8)
        place = lax.rem(i // 2 % 2 + shift[1], 2) * 2 + z % 2
        to_g = (z // 2) * 2 + lax.rem(core + shift[2], 2)
        return to_g * 4 + place, {"grid": to_g, "pts": probe * 4 + place}

    barrier = pltpu.get_barrier_semaphore()
    for peer, shifts in ((line_peer, line_shifts), (pts_peer, pts_shifts)):
        for shift in shifts:
            pl.semaphore_signal(barrier, inc=1, device_id=peer(shift)[1], device_id_type=pl.DeviceIdType.MESH)

    loads = [
        pltpu.make_async_copy(source, target, load_sem.at[n])
        for n, (source, target) in enumerate(
            (
                (owner_hbm, owner_ref), (slot_hbm, slot_ref), (count_hbm, count_ref),
                (probe_hbm, probe_ref), (weight_hbm, weight_ref), (scale_hbm, scale_ref),
            )
        )
    ]
    for load in loads:
        load.start()

    def start(sem, me, peer, shifts, source, target):
        for shift in shifts:
            k, device = peer(shift)
            pltpu.make_async_remote_copy(
                src_ref=source.at[k],
                dst_ref=target.at[me],
                send_sem=send_sem.at[sem],
                recv_sem=recv_sem.at[sem],
                device_id=device,
                device_id_type=pl.DeviceIdType.MESH,
            ).start()
        target[me] = source[me]

    def whole(sem, source, target):
        return pltpu.make_async_remote_copy(
            src_ref=source.at[pl.ds(0, PEERS - 1)],
            dst_ref=target.at[pl.ds(0, PEERS - 1)],
            send_sem=send_sem.at[sem],
            recv_sem=recv_sem.at[sem],
            device_id={"grid": g, "pts": i},
            device_id_type=pl.DeviceIdType.MESH,
        )

    for load in loads:
        load.wait()
    ell = jnp.full((1, 1), scale_ref[0], F32)
    lane8 = iota((8, 128), 1)

    used = [jnp.int32(0)] * 4
    lane512 = iota((8, 512), 1)
    probe_row = iota((8, 512), 0) == lane512 // 64
    blocks = probe_ref.shape[0]
    for b in range(blocks):
        owner = owner_ref[0, b]
        slot = slot_ref[0, b]
        column = owner // 8
        rank = jnp.int32(0)
        for c in range(4):
            here = column == c
            rank = jnp.where(here, used[c], rank)
            used[c] = used[c] + here.astype(I32)
        place = column * 16 + rank
        brick_y = (owner % 8) * 4 + slot // 32
        brick_z = slot % 32
        masked = jnp.where(lane8 < count_ref[0, b], probe_ref[b].astype(F32), 0.0).astype(BF16)
        padded = jnp.concatenate([weight_ref[b], jnp.zeros((64, 128), BF16)], axis=0)
        block_sum = lax.dot_general(masked, padded, (((1,), (1,)), ((), ())), preferred_element_type=F32)
        block_sum = jnp.where(lane8 == 64, brick_y.astype(F32), block_sum)
        block_sum = jnp.where(lane8 == 65, brick_z.astype(F32), block_sum)
        sums[pl.ds(b * 8, 8), :] = block_sum
        chosen = probe_row & (lane512 % 64 == place)
        sel[pl.ds(b * 8, 8), :] = chosen.astype(F32)

    spread = sel[...].T.astype(BF16)
    message = dot(spread, sums[...].astype(BF16))
    send1[...] = message.astype(BF16).reshape(PEERS, 16, 128)

    pl.semaphore_wait(barrier, 2 * (PEERS - 1))
    start(0, i, pts_peer, pts_shifts, send1, recv1)

    row_z, lane_z = iota((128, 256), 0), iota((128, 256), 1)
    value, slope = matern(jnp.abs(swapped(row_z) - swapped(lane_z % 128)).astype(F32), ell)
    along_z = jnp.concatenate(split(jnp.where(lane_z < 128, value, slope)), axis=0)
    row_y, lane_y = iota((256, 128), 0), iota((256, 128), 1)
    value, slope = matern(jnp.abs(swapped(row_y % 128) - swapped(lane_y)).astype(F32), ell)
    along_y = jnp.concatenate(split(jnp.where(row_y < 128, value, slope)), axis=1)
    row_x, lane_x = iota((256, 256), 0), iota((256, 256), 1)
    x_out = (row_x // 8) * 4 + row_x % 4
    x_in = (lane_x // 8) * 4 + lane_x % 4
    value, slope = matern(jnp.abs(x_out - x_in).astype(F32), ell)
    out_slope = (row_x // 4) % 2
    in_mixed = (lane_x // 4) % 2
    table_x = jnp.where(out_slope == in_mixed, value, jnp.where(out_slope == 1, slope, 0.0))
    along_x = jnp.concatenate(split(table_x), axis=1)

    whole(0, send1, recv1).wait_recv()

    arrived = recv1[...].reshape(PEERS * 16, 128)
    wide = arrived.astype(F32)
    brick_y = wide[:, 64:65].astype(I32)
    brick_z = wide[:, 65:66].astype(I32)
    lane_s = iota((PEERS * 16, 128), 1)
    is_z = brick_z == lane_s % 32
    is_y = (brick_y == lane_s).astype(F32)
    is_y_across = is_y.T[0:32].astype(BF16)
    is_y = is_y.astype(BF16)
    cell = iota((128, 256), 0)
    lane = iota((128, 256), 1)
    is_z2 = jnp.concatenate([is_z, is_z], axis=1)
    for t in range(8):
        copies = (cell == t * 8 + lane // 32).astype(F32).astype(BF16)
        placed = jnp.where(is_z2, dot(arrived, copies), 0.0).astype(BF16)
        rows = dot(is_y_across, placed)
        lines[pl.ds(t * 64, 32), :] = rows[:, 0:128]
        lines[pl.ds(t * 64 + 32, 32), :] = rows[:, 128:256]

    cells = lines[...].astype(BF16)
    by_z = dot(jnp.concatenate([cells, cells], axis=1), along_z).astype(BF16)
    for cx in range(4):
        part = by_z[cx * 128 : (cx + 1) * 128]
        by_y = dot(along_y, jnp.concatenate([part, part], axis=0))
        field[pl.ds(cx, 128, stride=8), :] = by_y[0:128, 0:128]
        field[pl.ds(4 + cx, 128, stride=8), :] = by_y[0:128, 128:256] + by_y[128:256, 0:128]
    for c in range(chunks):
        for k in range(per):
            cy = c * per + k
            send2[c, :, k] = field[pl.ds(cy * 256, 256), :].reshape(PEERS, 8, 128).astype(BF16)
        start(1 + c, mine, line_peer, line_shifts, send2.at[c], recv2.at[c])

    for c in range(chunks):
        whole(1 + c, send2.at[c], recv2.at[c]).wait_recv()
        for k in range(per):
            part = recv2[c, :, k].astype(F32).reshape(256, 128).astype(BF16)
            by_x = dot(along_x, jnp.concatenate([part, part], axis=0))
            send3[c, :, k] = by_x.reshape(PEERS, 8, 128).astype(BF16)
        start(1 + chunks + c, mine, line_peer, line_shifts, send3.at[c], recv3.at[c])

    is_y32 = is_y[:, 0:32]
    row2, lane2 = iota((256, 128), 0), iota((256, 128), 1)
    for c in range(chunks):
        whole(1 + chunks + c, send3.at[c], recv3.at[c]).wait_recv()
        for k in range(per):
            cy = c * per + k
            field[pl.ds(cy * 256, 256), :] = recv3[c, :, k].astype(F32).reshape(256, 128)
            gathered = jnp.zeros((PEERS * 16, 128), F32)
            for w in (0, 2, 4, 6):
                pair = [field[pl.ds(cy * 256 + w + u, 32, stride=8), :] for u in range(2)]
                rows = jnp.concatenate(pair, axis=1).astype(BF16)
                taken = jnp.where(is_z2, dot(is_y32, rows), 0.0).astype(BF16)
                cell_of = (w + row2 // 128) * 16 + cy * 4 + row2 % 128 // 32
                gathered = gathered + dot(taken, (lane2 == cell_of).astype(F32).astype(BF16))
            if cy == 0:
                total[...] = gathered
            elif cy < 3:
                total[...] = total[...] + gathered
            else:
                send4[...] = (total[...] + gathered).astype(BF16).reshape(PEERS, 16, 128)
    last = 1 + 2 * chunks
    start(last, i, pts_peer, pts_shifts, send4, recv4)
    whole(0, send1, recv1).wait_send()
    for c in range(chunks):
        whole(1 + c, send2.at[c], recv2.at[c]).wait_send()
        whole(1 + chunks + c, send3.at[c], recv3.at[c]).wait_send()
    whole(last, send4, recv4).wait_recv()
    rows_ref[...] = dot(sel[...].astype(BF16), recv4[...].reshape(PEERS * 16, 128))
    whole(last, send4, recv4).wait_send()


def points_kernel(count_ref, rows_ref, weight_ref, cov_ref, adj_ref):
    lane8 = iota((8, 128), 1)
    for b in range(weight_ref.shape[0]):
        block = rows_ref[pl.ds(b * 8, 8), :]
        both = jnp.concatenate([jnp.where(lane8 < 64, block, 0.0), jnp.where(lane8 < 64, 0.0, block)], axis=0)
        twice = jnp.concatenate([weight_ref[b], weight_ref[b]], axis=0)
        result = dot(both.astype(BF16), twice)
        usable = lane8 < count_ref[0, b]
        cov_ref[b] = jnp.where(usable, result[0:8], 0.0)
        adj_ref[b] = jnp.where(usable, result[8:16], 0.0)


CHUNKS = 4


def on_device(probes, weights, brick_owner, brick_slot, counts, length_scale):
    blocks = probes.shape[1]
    chunks = CHUNKS
    smem = pl.BlockSpec(memory_space=pltpu.SMEM)
    vmem = pl.BlockSpec(memory_space=pltpu.VMEM)
    small = pltpu.VMEM((PEERS, 16, 128), BF16)
    large = pltpu.VMEM((chunks, PEERS, 4 // chunks, 8, 128), BF16)
    rows = pl.pallas_call(
        functools.partial(kernel, chunks),
        out_shape=jax.ShapeDtypeStruct((blocks * 8, 128), F32),
        in_specs=[pl.BlockSpec(memory_space=pl.ANY)] * 6,
        out_specs=vmem,
        scratch_shapes=[
            pltpu.SMEM((1, blocks), I32),
            pltpu.SMEM((1, blocks), I32),
            pltpu.SMEM((1, blocks), I32),
            pltpu.SMEM((1,), F32),
            pltpu.VMEM(probes.shape[1:], BF16),
            pltpu.VMEM(weights.shape[1:], BF16),
            pltpu.VMEM((256, 128), F32),
            pltpu.VMEM((256, 512), F32),
            pltpu.VMEM((512, 128), F32),
            pltpu.VMEM((1024, 128), F32),
            pltpu.VMEM((512, 128), F32),
            small, small, large, large, large, large, small, small,
            pltpu.SemaphoreType.DMA((2 + 2 * chunks,)),
            pltpu.SemaphoreType.DMA((2 + 2 * chunks,)),
            pltpu.SemaphoreType.DMA((6,)),
        ],
        compiler_params=pltpu.CompilerParams(collective_id=0, has_side_effects=True, vmem_limit_bytes=24 << 20),
        name="covariance",
    )(
        *(
            pltpu.with_memory_space_constraint(a, pltpu.HBM)
            for a in (brick_owner.reshape(1, blocks), brick_slot, counts, probes[0], weights[0])
        ),
        length_scale,
    )
    out = jax.ShapeDtypeStruct((blocks, 8, 128), F32)
    cov, adj = pl.pallas_call(
        points_kernel,
        out_shape=(out, out),
        in_specs=[smem, vmem, vmem],
        out_specs=(vmem, vmem),
        compiler_params=pltpu.CompilerParams(vmem_limit_bytes=16 << 20),
        name="points",
    )(counts, rows, weights[0])
    return cov[None], adj[None]


def solution(mesh):
    placed = (
        P("grid", "pts", None, None),
        P("grid", "pts", None, None),
        P("grid", "pts", None),
        P("grid", "pts"),
        P("grid", "pts"),
        P(),
    )
    return jax.shard_map(
        on_device,
        mesh=mesh,
        in_specs=placed,
        out_specs=(P("grid", "pts", None, None), P("grid", "pts", None, None)),
        check_vma=False,
    )
```

```python
import functools
import math

import jax
import jax.numpy as jnp
from jax import lax
from jax.experimental import pallas as pl
from jax.experimental.pallas import tpu as pltpu
from jax.sharding import PartitionSpec as P

EXTENT = 128
ROOT_FIVE = math.sqrt(5.0)
F32 = jnp.float32
BF16 = jnp.bfloat16
I32 = jnp.int32
PEERS = 32


def iota(shape, dim):
    return lax.broadcasted_iota(I32, shape, dim)


def matern(distance, ell):
    scaled = (ROOT_FIVE / EXTENT) * distance / ell
    scale = jnp.exp(-scaled) * lax.rsqrt(EXTENT * ell)
    poly = 1.0 + scaled + scaled * scaled * (1.0 / 3.0)
    value = poly * scale
    slope = (scaled * scaled * (1.0 + scaled) * (1.0 / 3.0) - 0.5 * poly) * scale
    return value, slope


def split(table):
    high = table.astype(BF16)
    low = (table - high.astype(F32)).astype(BF16)
    return high, low


def swapped(place):
    return 4 * (place % 32) + place // 32


def dot(a, b):
    return jnp.dot(a, b, preferred_element_type=F32)


def kernel(
    chunks, owner_hbm, slot_hbm, count_hbm, probe_hbm, weight_hbm, scale_hbm, rows_ref, usable_ref,
    owner_ref, slot_ref, count_ref, scale_ref, probe_ref, weight_ref, sums, sel, slots, placed, lines, field, gather, total,
    send1, recv1, send2, recv2, send3, recv3, send4, recv4,
    send_sem, recv_sem, load_sem,
):
    g = lax.axis_index("grid")
    i = lax.axis_index("pts")
    probe = i // 4
    mine = g * 4 + i % 4
    at_z, core = (g // 2) * 2 + i % 2, g % 2
    per = 4 // chunks

    def hops(shift, size):
        return min(shift, size - shift)

    def farthest(sizes):
        shifts = [()]
        for size in sizes:
            shifts = [old + (new,) for old in shifts for new in range(size)]
        return shifts

    pts_shifts = sorted(farthest((4, 4, 2))[1:], key=lambda s: -hops(s[0], 4) - hops(s[1], 4) - s[2])
    line_shifts = sorted(farthest((8, 2, 2))[1:], key=lambda s: -hops(s[0], 8) - s[1] - 0.1 * s[2])

    def pts_peer(shift):
        to = lax.rem(i // 8 + shift[0], 4) * 8 + lax.rem(i // 2 % 4 + shift[1], 4) * 2 + lax.rem(i % 2 + shift[2], 2)
        return to, {"grid": g, "pts": to}

    def line_peer(shift):
        z = lax.rem(at_z + shift[0], 8)
        place = lax.rem(i // 2 % 2 + shift[1], 2) * 2 + z % 2
        to_g = (z // 2) * 2 + lax.rem(core + shift[2], 2)
        return to_g * 4 + place, {"grid": to_g, "pts": probe * 4 + place}

    barrier = pltpu.get_barrier_semaphore()
    for peer, shifts in ((line_peer, line_shifts), (pts_peer, pts_shifts)):
        for shift in shifts:
            pl.semaphore_signal(barrier, inc=1, device_id=peer(shift)[1], device_id_type=pl.DeviceIdType.MESH)

    loads = [
        pltpu.make_async_copy(source, target, load_sem.at[n])
        for n, (source, target) in enumerate(
            (
                (owner_hbm, owner_ref), (slot_hbm, slot_ref), (count_hbm, count_ref),
                (probe_hbm, probe_ref), (weight_hbm, weight_ref), (scale_hbm, scale_ref),
            )
        )
    ]
    for load in loads:
        load.start()

    def start(sem, me, peer, shifts, source, target):
        for shift in shifts:
            k, device = peer(shift)
            pltpu.make_async_remote_copy(
                src_ref=source.at[k],
                dst_ref=target.at[me],
                send_sem=send_sem.at[sem],
                recv_sem=recv_sem.at[sem],
                device_id=device,
                device_id_type=pl.DeviceIdType.MESH,
            ).start()
        target[me] = source[me]

    def whole(sem, source, target):
        return pltpu.make_async_remote_copy(
            src_ref=source.at[pl.ds(0, PEERS - 1)],
            dst_ref=target.at[pl.ds(0, PEERS - 1)],
            send_sem=send_sem.at[sem],
            recv_sem=recv_sem.at[sem],
            device_id={"grid": g, "pts": i},
            device_id_type=pl.DeviceIdType.MESH,
        )

    for load in loads:
        load.wait()
    ell = jnp.full((1, 1), scale_ref[0, 0], F32)
    lane8 = iota((8, 128), 1)

    used = [jnp.int32(0)] * 4
    lane512 = iota((8, 512), 1)
    probe_row = iota((8, 512), 0) == lane512 // 64
    blocks = probe_ref.shape[0]
    for b in range(blocks):
        owner = owner_ref[0, b]
        slot = slot_ref[0, b]
        column = owner // 8
        rank = jnp.int32(0)
        for c in range(4):
            here = column == c
            rank = jnp.where(here, used[c], rank)
            used[c] = used[c] + here.astype(I32)
        place = column * 16 + rank
        brick_y = (owner % 8) * 4 + slot // 32
        brick_z = slot % 32
        usable = lane8 < count_ref[0, b]
        usable_ref[b] = usable.astype(F32)
        masked = jnp.where(usable, probe_ref[b].astype(F32), 0.0).astype(BF16)
        padded = jnp.concatenate([weight_ref[b], jnp.zeros((64, 128), BF16)], axis=0)
        block_sum = lax.dot_general(masked, padded, (((1,), (1,)), ((), ())), preferred_element_type=F32)
        block_sum = jnp.where(lane8 == 64, brick_y.astype(F32), block_sum)
        block_sum = jnp.where(lane8 == 65, brick_z.astype(F32), block_sum)
        sums[pl.ds(b * 8, 8), :] = block_sum
        chosen = probe_row & (lane512 % 64 == place)
        sel[pl.ds(b * 8, 8), :] = chosen.astype(F32)

    spread = sel[...].T.astype(BF16)
    message = dot(spread, sums[...].astype(BF16))
    send1[...] = message.astype(BF16).reshape(PEERS, 16, 128)

    pl.semaphore_wait(barrier, 2 * (PEERS - 1))
    start(0, i, pts_peer, pts_shifts, send1, recv1)

    row_z, lane_z = iota((128, 256), 0), iota((128, 256), 1)
    value, slope = matern(jnp.abs(swapped(row_z) - swapped(lane_z % 128)).astype(F32), ell)
    along_z = jnp.concatenate(split(jnp.where(lane_z < 128, value, slope)), axis=0)
    row_y, lane_y = iota((256, 128), 0), iota((256, 128), 1)
    value, slope = matern(jnp.abs(swapped(row_y % 128) - swapped(lane_y)).astype(F32), ell)
    along_y = jnp.concatenate(split(jnp.where(row_y < 128, value, slope)), axis=1)
    row_x, lane_x = iota((256, 256), 0), iota((256, 256), 1)
    x_out = (row_x // 8) * 4 + row_x % 4
    x_in = (lane_x // 8) * 4 + lane_x % 4
    value, slope = matern(jnp.abs(x_out - x_in).astype(F32), ell)
    out_slope = (row_x // 4) % 2
    in_mixed = (lane_x // 4) % 2
    table_x = jnp.where(out_slope == in_mixed, value, jnp.where(out_slope == 1, slope, 0.0))
    along_x = jnp.concatenate(split(table_x), axis=1)

    whole(0, send1, recv1).wait_recv()

    wide = recv1[...].reshape(PEERS * 16, 128).astype(F32)
    brick_y = wide[:, 64:65].astype(I32)
    brick_z = wide[:, 65:66].astype(I32)
    across = wide.T[0:64].astype(BF16)
    lane256 = iota((PEERS * 16, 256), 1)
    brick = brick_y * 32 + brick_z
    for t in range(4):
        there = (lane256 == brick - t * 256).astype(F32).astype(BF16)
        cells = dot(across, there)
        placed[pl.ds(t * 128, 64), :] = cells[:, 0:128]
        placed[pl.ds(t * 128 + 64, 64), :] = cells[:, 128:256]
    group = iota((16, 128), 1) // 32
    for t in range(8):
        parts = [placed[pl.ds(t * 64 + cz, 16, stride=4), :] for cz in range(4)]
        for u in range(4):
            turned = [parts[cz] if cz == u else pltpu.roll(parts[cz], (cz - u) % 4 * 32, 1) for cz in range(4)]
            row = jnp.where(
                group < 2, jnp.where(group == 0, turned[0], turned[1]), jnp.where(group == 2, turned[2], turned[3])
            )
            lines[pl.ds(t * 4 + u, 16, stride=32), :] = row

    cells = lines[...].astype(BF16)
    by_z = dot(jnp.concatenate([cells, cells], axis=1), along_z).astype(BF16)
    for cx in range(4):
        part = by_z[cx * 128 : (cx + 1) * 128]
        by_y = dot(along_y, jnp.concatenate([part, part], axis=0))
        field[pl.ds(cx, 128, stride=8), :] = by_y[0:128, 0:128]
        field[pl.ds(4 + cx, 128, stride=8), :] = by_y[0:128, 128:256] + by_y[128:256, 0:128]
    for c in range(chunks):
        for k in range(per):
            cy = c * per + k
            send2[c, :, k] = field[pl.ds(cy * 256, 256), :].reshape(PEERS, 8, 128).astype(BF16)
        start(1 + c, mine, line_peer, line_shifts, send2.at[c], recv2.at[c])

    lane_s = iota((PEERS * 16, 128), 1)
    is_z = brick_z == lane_s % 32
    is_y32 = (brick_y == lane_s).astype(F32).astype(BF16)[:, 0:32]
    is_z2 = jnp.concatenate([is_z, is_z], axis=1)
    place, lane = iota((1024, 128), 0), iota((1024, 128), 1)
    for cy in range(4):
        gather[cy] = (lane == place // 128 * 16 + cy * 4 + place % 128 // 32).astype(F32).astype(BF16)
    slots[...] = sel[...].astype(BF16)

    for c in range(chunks):
        whole(1 + c, send2.at[c], recv2.at[c]).wait_recv()
        for k in range(per):
            part = recv2[c, :, k].astype(F32).reshape(256, 128).astype(BF16)
            by_x = dot(along_x, jnp.concatenate([part, part], axis=0))
            send3[c, :, k] = by_x.reshape(PEERS, 8, 128).astype(BF16)
        start(1 + chunks + c, mine, line_peer, line_shifts, send3.at[c], recv3.at[c])

    for c in range(chunks):
        whole(1 + chunks + c, send3.at[c], recv3.at[c]).wait_recv()
        for k in range(per):
            cy = c * per + k
            field[pl.ds(cy * 256, 256), :] = recv3[c, :, k].astype(F32).reshape(256, 128)
            taken = []
            for w in (0, 2, 4, 6):
                pair = [field[pl.ds(cy * 256 + w + u, 32, stride=8), :] for u in range(2)]
                rows = jnp.concatenate(pair, axis=1).astype(BF16)
                taken.append(jnp.where(is_z2, dot(is_y32, rows), 0.0).astype(BF16))
            gathered = dot(jnp.concatenate(taken, axis=1), gather[cy])
            if cy == 0:
                total[...] = gathered
            elif cy < 3:
                total[...] = total[...] + gathered
            else:
                send4[...] = (total[...] + gathered).astype(BF16).reshape(PEERS, 16, 128)
    last = 1 + 2 * chunks
    start(last, i, pts_peer, pts_shifts, send4, recv4)
    whole(0, send1, recv1).wait_send()
    for c in range(chunks):
        whole(1 + c, send2.at[c], recv2.at[c]).wait_send()
        whole(1 + chunks + c, send3.at[c], recv3.at[c]).wait_send()
    whole(last, send4, recv4).wait_recv()
    rows_ref[...] = dot(slots[...], recv4[...].reshape(PEERS * 16, 128))
    whole(last, send4, recv4).wait_send()


def points_kernel(usable_ref, rows_ref, weight_ref, cov_ref, adj_ref):
    lane8 = iota((8, 128), 1)
    for b in range(weight_ref.shape[0]):
        block = rows_ref[pl.ds(b * 8, 8), :]
        both = jnp.concatenate([jnp.where(lane8 < 64, block, 0.0), jnp.where(lane8 < 64, 0.0, block)], axis=0)
        twice = jnp.concatenate([weight_ref[b], weight_ref[b]], axis=0)
        result = dot(both.astype(BF16), twice)
        usable = usable_ref[b] > 0.0
        cov_ref[b] = jnp.where(usable, result[0:8], 0.0)
        adj_ref[b] = jnp.where(usable, result[8:16], 0.0)


CHUNKS = 4


def on_device(probes, weights, brick_owner, brick_slot, counts, length_scale):
    blocks = probes.shape[1]
    chunks = CHUNKS
    vmem = pl.BlockSpec(memory_space=pltpu.VMEM)
    small = pltpu.VMEM((PEERS, 16, 128), BF16)
    large = pltpu.VMEM((chunks, PEERS, 4 // chunks, 8, 128), BF16)
    rows, usable = pl.pallas_call(
        functools.partial(kernel, chunks),
        out_shape=(jax.ShapeDtypeStruct((blocks * 8, 128), F32), jax.ShapeDtypeStruct((blocks, 8, 128), F32)),
        in_specs=[pl.BlockSpec(memory_space=pl.ANY)] * 6,
        out_specs=(vmem, vmem),
        scratch_shapes=[
            pltpu.SMEM((1, blocks), I32),
            pltpu.SMEM((1, blocks), I32),
            pltpu.SMEM((1, blocks), I32),
            pltpu.SMEM((1, 1), F32),
            pltpu.VMEM(probes.shape[1:], BF16),
            pltpu.VMEM(weights.shape[1:], BF16),
            pltpu.VMEM((256, 128), F32),
            pltpu.VMEM((256, 512), F32),
            pltpu.VMEM((256, 512), BF16),
            pltpu.VMEM((512, 128), F32),
            pltpu.VMEM((512, 128), F32),
            pltpu.VMEM((1024, 128), F32),
            pltpu.VMEM((4, 1024, 128), BF16),
            pltpu.VMEM((512, 128), F32),
            small, small, large, large, large, large, small, small,
            pltpu.SemaphoreType.DMA((2 + 2 * chunks,)),
            pltpu.SemaphoreType.DMA((2 + 2 * chunks,)),
            pltpu.SemaphoreType.DMA((6,)),
        ],
        compiler_params=pltpu.CompilerParams(collective_id=0, has_side_effects=True, vmem_limit_bytes=24 << 20),
        name="covariance",
    )(
        *(
            pltpu.with_memory_space_constraint(a, pltpu.HBM)
            for a in (brick_owner.reshape(1, blocks), brick_slot, counts, probes[0], weights[0])
        ),
        length_scale,
    )
    out = jax.ShapeDtypeStruct((blocks, 8, 128), F32)
    cov, adj = pl.pallas_call(
        points_kernel,
        out_shape=(out, out),
        in_specs=[vmem, vmem, vmem],
        out_specs=(vmem, vmem),
        compiler_params=pltpu.CompilerParams(vmem_limit_bytes=16 << 20),
        name="points",
    )(usable, rows, weights[0])
    return cov[None], adj[None]


def solution(mesh):
    placed = (
        P("grid", "pts", None, None),
        P("grid", "pts", None, None),
        P("grid", "pts", None),
        P("grid", "pts"),
        P("grid", "pts"),
        P("grid", "pts"),
    )
    sharded = jax.shard_map(
        on_device,
        mesh=mesh,
        in_specs=placed,
        out_specs=(P("grid", "pts", None, None), P("grid", "pts", None, None)),
        check_vma=False,
    )

    def run(probes, weights, brick_owner, brick_slot, counts, length_scale):
        spread = jnp.broadcast_to(length_scale[None, :], brick_owner.shape[:1] + (mesh.shape["pts"],))
        return sharded(probes, weights, brick_owner, brick_slot, counts, spread)

    return run
```

```python
import functools
import math

import jax
import jax.numpy as jnp
from jax import lax
from jax.experimental import pallas as pl
from jax.experimental.pallas import tpu as pltpu
from jax.sharding import PartitionSpec as P

EXTENT = 128
ROOT_FIVE = math.sqrt(5.0)
F32 = jnp.float32
BF16 = jnp.bfloat16
I32 = jnp.int32
PEERS = 32


def iota(shape, dim):
    return lax.broadcasted_iota(I32, shape, dim)


def matern(distance, ell):
    scaled = (ROOT_FIVE / EXTENT) * distance / ell
    scale = jnp.exp(-scaled) * lax.rsqrt(EXTENT * ell)
    poly = 1.0 + scaled + scaled * scaled * (1.0 / 3.0)
    value = poly * scale
    slope = (scaled * scaled * (1.0 + scaled) * (1.0 / 3.0) - 0.5 * poly) * scale
    return value, slope


def split(table):
    high = table.astype(BF16)
    low = (table - high.astype(F32)).astype(BF16)
    return high, low


def swapped(place):
    return 4 * (place % 32) + place // 32


def dot(a, b):
    return jnp.dot(a, b, preferred_element_type=F32)


def kernel(
    chunks, owner_hbm, slot_hbm, count_hbm, probe_hbm, weight_hbm, scale_hbm, rows_ref, usable_ref,
    owner_ref, slot_ref, count_ref, scale_ref, probe_ref, weight_ref, sums, sel, slots, placed, lines, field, gather, total,
    send1, recv1, send2, recv2, send3, recv3, send4, recv4,
    send_sem, recv_sem, load_sem,
):
    g = lax.axis_index("grid")
    i = lax.axis_index("pts")
    probe = i // 4
    mine = g * 4 + i % 4
    at_z, core = (g // 2) * 2 + i % 2, g % 2
    per = 4 // chunks

    def hops(shift, size):
        return min(shift, size - shift)

    def farthest(sizes):
        shifts = [()]
        for size in sizes:
            shifts = [old + (new,) for old in shifts for new in range(size)]
        return shifts

    pts_shifts = sorted(farthest((4, 4, 2))[1:], key=lambda s: -hops(s[0], 4) - hops(s[1], 4) - s[2])
    line_shifts = sorted(farthest((8, 2, 2))[1:], key=lambda s: -hops(s[0], 8) - s[1] - 0.1 * s[2])

    def pts_peer(shift):
        to = lax.rem(i // 8 + shift[0], 4) * 8 + lax.rem(i // 2 % 4 + shift[1], 4) * 2 + lax.rem(i % 2 + shift[2], 2)
        return to, {"grid": g, "pts": to}

    def line_peer(shift):
        z = lax.rem(at_z + shift[0], 8)
        place = lax.rem(i // 2 % 2 + shift[1], 2) * 2 + z % 2
        to_g = (z // 2) * 2 + lax.rem(core + shift[2], 2)
        return to_g * 4 + place, {"grid": to_g, "pts": probe * 4 + place}

    barrier = pltpu.get_barrier_semaphore()
    for peer, shifts in ((line_peer, line_shifts), (pts_peer, pts_shifts)):
        for shift in shifts:
            pl.semaphore_signal(barrier, inc=1, device_id=peer(shift)[1], device_id_type=pl.DeviceIdType.MESH)

    loads = [
        pltpu.make_async_copy(source, target, load_sem.at[n])
        for n, (source, target) in enumerate(
            (
                (owner_hbm, owner_ref), (slot_hbm, slot_ref), (count_hbm, count_ref),
                (probe_hbm, probe_ref), (weight_hbm, weight_ref), (scale_hbm, scale_ref),
            )
        )
    ]
    for load in loads:
        load.start()

    def start(sem, me, peer, shifts, source, target):
        for shift in shifts:
            k, device = peer(shift)
            pltpu.make_async_remote_copy(
                src_ref=source.at[k],
                dst_ref=target.at[me],
                send_sem=send_sem.at[sem],
                recv_sem=recv_sem.at[sem],
                device_id=device,
                device_id_type=pl.DeviceIdType.MESH,
            ).start()
        target[me] = source[me]

    def whole(sem, source, target):
        return pltpu.make_async_remote_copy(
            src_ref=source.at[pl.ds(0, PEERS - 1)],
            dst_ref=target.at[pl.ds(0, PEERS - 1)],
            send_sem=send_sem.at[sem],
            recv_sem=recv_sem.at[sem],
            device_id={"grid": g, "pts": i},
            device_id_type=pl.DeviceIdType.MESH,
        )

    for load in loads:
        load.wait()
    ell = jnp.full((1, 1), scale_ref[0, 0], F32)
    lane8 = iota((8, 128), 1)

    used = [jnp.int32(0)] * 4
    lane512 = iota((8, 512), 1)
    probe_row = iota((8, 512), 0) == lane512 // 64
    blocks = probe_ref.shape[0]
    for b in range(blocks):
        owner = owner_ref[0, b]
        slot = slot_ref[0, b]
        column = owner // 8
        rank = jnp.int32(0)
        for c in range(4):
            here = column == c
            rank = jnp.where(here, used[c], rank)
            used[c] = used[c] + here.astype(I32)
        place = column * 16 + rank
        brick_y = (owner % 8) * 4 + slot // 32
        brick_z = slot % 32
        usable = lane8 < count_ref[0, b]
        usable_ref[b] = usable.astype(F32)
        masked = jnp.where(usable, probe_ref[b].astype(F32), 0.0).astype(BF16)
        padded = jnp.concatenate([weight_ref[b], jnp.zeros((64, 128), BF16)], axis=0)
        block_sum = lax.dot_general(masked, padded, (((1,), (1,)), ((), ())), preferred_element_type=F32)
        block_sum = jnp.where(lane8 == 64, brick_y.astype(F32), block_sum)
        block_sum = jnp.where(lane8 == 65, brick_z.astype(F32), block_sum)
        sums[pl.ds(b * 8, 8), :] = block_sum
        chosen = probe_row & (lane512 % 64 == place)
        sel[pl.ds(b * 8, 8), :] = chosen.astype(F32)

    spread = sel[...].T.astype(BF16)
    message = dot(spread, sums[...].astype(BF16))
    send1[...] = message.astype(BF16).reshape(PEERS, 16, 128)

    pl.semaphore_wait(barrier, 2 * (PEERS - 1))
    start(0, i, pts_peer, pts_shifts, send1, recv1)

    row_z, lane_z = iota((128, 256), 0), iota((128, 256), 1)
    value, slope = matern(jnp.abs(swapped(row_z) - swapped(lane_z % 128)).astype(F32), ell)
    along_z = jnp.concatenate(split(jnp.where(lane_z < 128, value, slope)), axis=0)
    row_y, lane_y = iota((256, 128), 0), iota((256, 128), 1)
    value, slope = matern(jnp.abs(swapped(row_y % 128) - swapped(lane_y)).astype(F32), ell)
    along_y = jnp.concatenate(split(jnp.where(row_y < 128, value, slope)), axis=1)
    row_x, lane_x = iota((256, 256), 0), iota((256, 256), 1)
    x_out = (row_x // 8) * 4 + row_x % 4
    x_in = (lane_x // 8) * 4 + lane_x % 4
    value, slope = matern(jnp.abs(x_out - x_in).astype(F32), ell)
    out_slope = (row_x // 4) % 2
    in_mixed = (lane_x // 4) % 2
    table_x = jnp.where(out_slope == in_mixed, value, jnp.where(out_slope == 1, slope, 0.0))
    along_x = jnp.concatenate(split(table_x), axis=1)

    whole(0, send1, recv1).wait_recv()

    wide = recv1[...].reshape(PEERS * 16, 128).astype(F32)
    brick_y = wide[:, 64:65].astype(I32)
    brick_z = wide[:, 65:66].astype(I32)
    across = wide.T[0:64].astype(BF16)
    brick = brick_y * 32 + brick_z - iota((PEERS * 16, 128), 1)
    for t in range(4):
        pair = [(brick == t * 256).astype(F32), (brick == t * 256 + 128).astype(F32)]
        there = jnp.concatenate(pair, axis=1).astype(BF16)
        cells = dot(across, there)
        placed[pl.ds(t * 128, 64), :] = cells[:, 0:128]
        placed[pl.ds(t * 128 + 64, 64), :] = cells[:, 128:256]
    group = iota((16, 128), 1) // 32
    for t in range(8):
        parts = [placed[pl.ds(t * 64 + cz, 16, stride=4), :] for cz in range(4)]
        for u in range(4):
            turned = [parts[cz] if cz == u else pltpu.roll(parts[cz], (cz - u) % 4 * 32, 1) for cz in range(4)]
            row = jnp.where(
                group < 2, jnp.where(group == 0, turned[0], turned[1]), jnp.where(group == 2, turned[2], turned[3])
            )
            lines[pl.ds(t * 4 + u, 16, stride=32), :] = row

    cells = lines[...].astype(BF16)
    by_z = dot(jnp.concatenate([cells, cells], axis=1), along_z).astype(BF16)
    for cx in range(4):
        part = by_z[cx * 128 : (cx + 1) * 128]
        by_y = dot(along_y, jnp.concatenate([part, part], axis=0))
        field[pl.ds(cx, 128, stride=8), :] = by_y[0:128, 0:128]
        field[pl.ds(4 + cx, 128, stride=8), :] = by_y[0:128, 128:256] + by_y[128:256, 0:128]
    for c in range(chunks):
        for k in range(per):
            cy = c * per + k
            send2[c, :, k] = field[pl.ds(cy * 256, 256), :].reshape(PEERS, 8, 128).astype(BF16)
        start(1 + c, mine, line_peer, line_shifts, send2.at[c], recv2.at[c])

    lane_s = iota((PEERS * 16, 128), 1)
    is_z = brick_z == lane_s % 32
    is_y32 = (brick_y == lane_s).astype(F32).astype(BF16)[:, 0:32]
    is_z2 = jnp.concatenate([is_z, is_z], axis=1)
    place, lane = iota((1024, 128), 0), iota((1024, 128), 1)
    for cy in range(4):
        gather[cy] = (lane == place // 128 * 16 + cy * 4 + place % 128 // 32).astype(F32).astype(BF16)
    slots[...] = sel[...].astype(BF16)

    for c in range(chunks):
        whole(1 + c, send2.at[c], recv2.at[c]).wait_recv()
        for k in range(per):
            part = recv2[c, :, k].astype(F32).reshape(256, 128).astype(BF16)
            by_x = dot(along_x, jnp.concatenate([part, part], axis=0))
            send3[c, :, k] = by_x.reshape(PEERS, 8, 128).astype(BF16)
        start(1 + chunks + c, mine, line_peer, line_shifts, send3.at[c], recv3.at[c])

    for c in range(chunks):
        whole(1 + chunks + c, send3.at[c], recv3.at[c]).wait_recv()
        for k in range(per):
            cy = c * per + k
            field[pl.ds(cy * 256, 256), :] = recv3[c, :, k].astype(F32).reshape(256, 128)
            taken = []
            for w in (0, 2, 4, 6):
                pair = [field[pl.ds(cy * 256 + w + u, 32, stride=8), :] for u in range(2)]
                rows = jnp.concatenate(pair, axis=1).astype(BF16)
                taken.append(jnp.where(is_z2, dot(is_y32, rows), 0.0).astype(BF16))
            gathered = dot(jnp.concatenate(taken, axis=1), gather[cy])
            if cy == 0:
                total[...] = gathered
            elif cy < 3:
                total[...] = total[...] + gathered
            else:
                send4[...] = (total[...] + gathered).astype(BF16).reshape(PEERS, 16, 128)
    last = 1 + 2 * chunks
    start(last, i, pts_peer, pts_shifts, send4, recv4)
    whole(0, send1, recv1).wait_send()
    for c in range(chunks):
        whole(1 + c, send2.at[c], recv2.at[c]).wait_send()
        whole(1 + chunks + c, send3.at[c], recv3.at[c]).wait_send()
    whole(last, send4, recv4).wait_recv()
    rows_ref[...] = dot(slots[...], recv4[...].reshape(PEERS * 16, 128))
    whole(last, send4, recv4).wait_send()


def points_kernel(usable_ref, rows_ref, weight_ref, cov_ref, adj_ref):
    lane8 = iota((8, 128), 1)
    left = lane8 < 64
    for b in range(0, weight_ref.shape[0], 2):
        first, second = rows_ref[pl.ds(b * 8, 8), :], rows_ref[pl.ds(b * 8 + 8, 8), :]
        four = jnp.concatenate(
            [
                jnp.where(left, first, 0.0), jnp.where(left, pltpu.roll(first, 64, 1), 0.0),
                jnp.where(left, 0.0, pltpu.roll(second, 64, 1)), jnp.where(left, 0.0, second),
            ],
            axis=0,
        )
        result = dot(four.astype(BF16), weight_ref[pl.ds(b, 2)].reshape(128, 128))
        for u in range(2):
            usable = usable_ref[b + u] > 0.0
            cov_ref[b + u] = jnp.where(usable, result[u * 16 : u * 16 + 8], 0.0)
            adj_ref[b + u] = jnp.where(usable, result[u * 16 + 8 : u * 16 + 16], 0.0)


CHUNKS = 4


def on_device(probes, weights, brick_owner, brick_slot, counts, length_scale):
    blocks = probes.shape[1]
    chunks = CHUNKS
    vmem = pl.BlockSpec(memory_space=pltpu.VMEM)
    small = pltpu.VMEM((PEERS, 16, 128), BF16)
    large = pltpu.VMEM((chunks, PEERS, 4 // chunks, 8, 128), BF16)
    rows, usable = pl.pallas_call(
        functools.partial(kernel, chunks),
        out_shape=(jax.ShapeDtypeStruct((blocks * 8, 128), F32), jax.ShapeDtypeStruct((blocks, 8, 128), F32)),
        in_specs=[pl.BlockSpec(memory_space=pl.ANY)] * 6,
        out_specs=(vmem, vmem),
        scratch_shapes=[
            pltpu.SMEM((1, blocks), I32),
            pltpu.SMEM((1, blocks), I32),
            pltpu.SMEM((1, blocks), I32),
            pltpu.SMEM((1, 1), F32),
            pltpu.VMEM(probes.shape[1:], BF16),
            pltpu.VMEM(weights.shape[1:], BF16),
            pltpu.VMEM((256, 128), F32),
            pltpu.VMEM((256, 512), F32),
            pltpu.VMEM((256, 512), BF16),
            pltpu.VMEM((512, 128), F32),
            pltpu.VMEM((512, 128), F32),
            pltpu.VMEM((1024, 128), F32),
            pltpu.VMEM((4, 1024, 128), BF16),
            pltpu.VMEM((512, 128), F32),
            small, small, large, large, large, large, small, small,
            pltpu.SemaphoreType.DMA((2 + 2 * chunks,)),
            pltpu.SemaphoreType.DMA((2 + 2 * chunks,)),
            pltpu.SemaphoreType.DMA((6,)),
        ],
        compiler_params=pltpu.CompilerParams(collective_id=0, has_side_effects=True, vmem_limit_bytes=24 << 20),
        name="covariance",
    )(
        *(
            pltpu.with_memory_space_constraint(a, pltpu.HBM)
            for a in (brick_owner.reshape(1, blocks), brick_slot, counts, probes[0], weights[0])
        ),
        length_scale,
    )
    out = jax.ShapeDtypeStruct((blocks, 8, 128), F32)
    cov, adj = pl.pallas_call(
        points_kernel,
        out_shape=(out, out),
        in_specs=[vmem, vmem, vmem],
        out_specs=(vmem, vmem),
        compiler_params=pltpu.CompilerParams(vmem_limit_bytes=16 << 20),
        name="points",
    )(usable, rows, weights[0])
    return cov[None], adj[None]


def solution(mesh):
    placed = (
        P("grid", "pts", None, None),
        P("grid", "pts", None, None),
        P("grid", "pts", None),
        P("grid", "pts"),
        P("grid", "pts"),
        P("grid", "pts"),
    )
    sharded = jax.shard_map(
        on_device,
        mesh=mesh,
        in_specs=placed,
        out_specs=(P("grid", "pts", None, None), P("grid", "pts", None, None)),
        check_vma=False,
    )

    def run(probes, weights, brick_owner, brick_slot, counts, length_scale):
        spread = jnp.broadcast_to(length_scale[None, :], brick_owner.shape[:1] + (mesh.shape["pts"],))
        return sharded(probes, weights, brick_owner, brick_slot, counts, spread)

    return run
```

```python
import functools
import math

import jax
import jax.numpy as jnp
from jax import lax
from jax.experimental import pallas as pl
from jax.experimental.pallas import tpu as pltpu
from jax.sharding import PartitionSpec as P

EXTENT = 128
ROOT_FIVE = math.sqrt(5.0)
F32 = jnp.float32
BF16 = jnp.bfloat16
I32 = jnp.int32
PEERS = 32
NEAR = ((2, 0), (6, 0), (2, 1), (6, 1), (0, 1))


def iota(shape, dim):
    return lax.broadcasted_iota(I32, shape, dim)


def matern(distance, ell):
    scaled = (ROOT_FIVE / EXTENT) * distance / ell
    scale = jnp.exp(-scaled) * lax.rsqrt(EXTENT * ell)
    poly = 1.0 + scaled + scaled * scaled * (1.0 / 3.0)
    value = poly * scale
    slope = (scaled * scaled * (1.0 + scaled) * (1.0 / 3.0) - 0.5 * poly) * scale
    return value, slope


def split(table):
    high = table.astype(BF16)
    low = (table - high.astype(F32)).astype(BF16)
    return high, low


def swapped(place):
    return 4 * (place % 32) + place // 32


def dot(a, b):
    return jnp.dot(a, b, preferred_element_type=F32)


def kernel(
    chunks, owner_hbm, slot_hbm, count_hbm, probe_hbm, weight_hbm, scale_hbm, rows_ref, usable_ref,
    owner_ref, slot_ref, count_ref, scale_ref, probe_ref, weight_ref, sums, sel, slots, placed, lines, field, gather, total,
    send1, recv1, send2, recv2, send3, recv3, send4, recv4,
    send_sem, recv_sem, load_sem, slab_sem, all_sem,
):
    g = lax.axis_index("grid")
    i = lax.axis_index("pts")
    probe = i // 4
    mine = g * 4 + i % 4
    at_z, core = (g // 2) * 2 + i % 2, g % 2
    per = 4 // chunks

    def hops(shift, size):
        return min(shift, size - shift)

    def farthest(sizes):
        shifts = [()]
        for size in sizes:
            shifts = [old + (new,) for old in shifts for new in range(size)]
        return shifts

    pts_shifts = sorted(farthest((4, 4, 2))[1:], key=lambda s: -hops(s[0], 4) - hops(s[1], 4) - s[2])
    line_shifts = sorted(farthest((8, 2, 2))[1:], key=lambda s: -hops(s[0], 8) - s[1] - 0.1 * s[2])

    def pts_peer(shift):
        to = lax.rem(i // 8 + shift[0], 4) * 8 + lax.rem(i // 2 % 4 + shift[1], 4) * 2 + lax.rem(i % 2 + shift[2], 2)
        return to, {"grid": g, "pts": to}

    def line_peer(shift):
        z = lax.rem(at_z + shift[0], 8)
        place = lax.rem(i // 2 % 2 + shift[1], 2) * 2 + z % 2
        to_g = (z // 2) * 2 + lax.rem(core + shift[2], 2)
        return to_g * 4 + place, {"grid": to_g, "pts": probe * 4 + place}

    near = [{"grid": lax.rem(g + hop, 8) // 2 * 2 + lax.rem(core + swap, 2), "pts": i} for hop, swap in NEAR]
    barrier = pltpu.get_barrier_semaphore()
    greeted = [pts_peer(shift)[1] for shift in pts_shifts[:16]] + near + [pts_peer(shift)[1] for shift in pts_shifts[16:]]
    for device in greeted:
        pl.semaphore_signal(barrier, inc=1, device_id=device, device_id_type=pl.DeviceIdType.MESH)

    loads = [
        pltpu.make_async_copy(source, target, load_sem.at[n])
        for n, (source, target) in enumerate(
            (
                (owner_hbm, owner_ref), (slot_hbm, slot_ref), (count_hbm, count_ref),
                (probe_hbm, probe_ref), (weight_hbm, weight_ref), (scale_hbm, scale_ref),
            )
        )
    ]
    for load in loads:
        load.start()

    def start(sem, me, peer, shifts, source, target):
        for shift in shifts:
            k, device = peer(shift)
            pltpu.make_async_remote_copy(
                src_ref=source.at[k],
                dst_ref=target.at[me],
                send_sem=send_sem.at[sem],
                recv_sem=recv_sem.at[sem],
                device_id=device,
                device_id_type=pl.DeviceIdType.MESH,
            ).start()
        target[me] = source[me]

    def whole(sem, source, target):
        return pltpu.make_async_remote_copy(
            src_ref=source.at[pl.ds(0, PEERS - 1)],
            dst_ref=target.at[pl.ds(0, PEERS - 1)],
            send_sem=send_sem.at[sem],
            recv_sem=recv_sem.at[sem],
            device_id={"grid": g, "pts": i},
            device_id_type=pl.DeviceIdType.MESH,
        )

    for load in loads:
        load.wait()
    ell = jnp.full((1, 1), scale_ref[0, 0], F32)
    lane8 = iota((8, 128), 1)

    used = [jnp.int32(0)] * 4
    lane512 = iota((8, 512), 1)
    probe_row = iota((8, 512), 0) == lane512 // 64
    blocks = probe_ref.shape[0]
    for b in range(blocks):
        owner = owner_ref[0, b]
        slot = slot_ref[0, b]
        column = owner // 8
        rank = jnp.int32(0)
        for c in range(4):
            here = column == c
            rank = jnp.where(here, used[c], rank)
            used[c] = used[c] + here.astype(I32)
        place = column * 16 + rank
        brick_y = (owner % 8) * 4 + slot // 32
        brick_z = slot % 32
        usable = lane8 < count_ref[0, b]
        usable_ref[b] = usable.astype(F32)
        masked = jnp.where(usable, probe_ref[b].astype(F32), 0.0).astype(BF16)
        padded = jnp.concatenate([weight_ref[b], jnp.zeros((64, 128), BF16)], axis=0)
        block_sum = lax.dot_general(masked, padded, (((1,), (1,)), ((), ())), preferred_element_type=F32)
        block_sum = jnp.where(lane8 == 64, brick_y.astype(F32), block_sum)
        block_sum = jnp.where(lane8 == 65, brick_z.astype(F32), block_sum)
        sums[pl.ds(b * 8, 8), :] = block_sum
        chosen = probe_row & (lane512 % 64 == place)
        sel[pl.ds(b * 8, 8), :] = chosen.astype(F32)

    spread = sel[...].T.astype(BF16)
    message = dot(spread, sums[...].astype(BF16))
    send1[...] = message.astype(BF16).reshape(PEERS, 16, 128)

    pl.semaphore_wait(barrier, PEERS - 1 + len(NEAR))
    start(0, i, pts_peer, pts_shifts, send1, recv1)
    for device in near:
        pl.semaphore_signal(slab_sem, inc=1, device_id=device, device_id_type=pl.DeviceIdType.MESH)

    row_z, lane_z = iota((128, 256), 0), iota((128, 256), 1)
    value, slope = matern(jnp.abs(swapped(row_z) - swapped(lane_z % 128)).astype(F32), ell)
    along_z = jnp.concatenate(split(jnp.where(lane_z < 128, value, slope)), axis=0)
    row_y, lane_y = iota((256, 128), 0), iota((256, 128), 1)
    value, slope = matern(jnp.abs(swapped(row_y % 128) - swapped(lane_y)).astype(F32), ell)
    along_y = jnp.concatenate(split(jnp.where(row_y < 128, value, slope)), axis=1)
    row_x, lane_x = iota((256, 256), 0), iota((256, 256), 1)
    x_out = (row_x // 8) * 4 + row_x % 4
    x_in = (lane_x // 8) * 4 + lane_x % 4
    value, slope = matern(jnp.abs(x_out - x_in).astype(F32), ell)
    out_slope = (row_x // 4) % 2
    in_mixed = (lane_x // 4) % 2
    table_x = jnp.where(out_slope == in_mixed, value, jnp.where(out_slope == 1, slope, 0.0))
    along_x = jnp.concatenate(split(table_x), axis=1)

    pl.semaphore_wait(slab_sem, len(NEAR))
    pl.semaphore_signal(all_sem, inc=1, device_id=near[0], device_id_type=pl.DeviceIdType.MESH)
    whole(0, send1, recv1).wait_recv()

    wide = recv1[...].reshape(PEERS * 16, 128).astype(F32)
    brick_y = wide[:, 64:65].astype(I32)
    brick_z = wide[:, 65:66].astype(I32)
    across = wide.T[0:64].astype(BF16)
    brick = brick_y * 32 + brick_z - iota((PEERS * 16, 128), 1)
    for t in range(4):
        pair = [(brick == t * 256).astype(F32), (brick == t * 256 + 128).astype(F32)]
        there = jnp.concatenate(pair, axis=1).astype(BF16)
        cells = dot(across, there)
        placed[pl.ds(t * 128, 64), :] = cells[:, 0:128]
        placed[pl.ds(t * 128 + 64, 64), :] = cells[:, 128:256]
    group = iota((16, 128), 1) // 32
    for t in range(8):
        parts = [placed[pl.ds(t * 64 + cz, 16, stride=4), :] for cz in range(4)]
        for u in range(4):
            turned = [parts[cz] if cz == u else pltpu.roll(parts[cz], (cz - u) % 4 * 32, 1) for cz in range(4)]
            row = jnp.where(
                group < 2, jnp.where(group == 0, turned[0], turned[1]), jnp.where(group == 2, turned[2], turned[3])
            )
            lines[pl.ds(t * 4 + u, 16, stride=32), :] = row

    cells = lines[...].astype(BF16)
    by_z = dot(jnp.concatenate([cells, cells], axis=1), along_z).astype(BF16)
    for cx in range(4):
        part = by_z[cx * 128 : (cx + 1) * 128]
        by_y = dot(along_y, jnp.concatenate([part, part], axis=0))
        field[pl.ds(cx, 128, stride=8), :] = by_y[0:128, 0:128]
        field[pl.ds(4 + cx, 128, stride=8), :] = by_y[0:128, 128:256] + by_y[128:256, 0:128]
    pl.semaphore_wait(all_sem, 1)
    for c in range(chunks):
        for k in range(per):
            cy = c * per + k
            send2[c, :, k] = field[pl.ds(cy * 256, 256), :].reshape(PEERS, 8, 128).astype(BF16)
        start(1 + c, mine, line_peer, line_shifts, send2.at[c], recv2.at[c])

    lane_s = iota((PEERS * 16, 128), 1)
    is_z = brick_z == lane_s % 32
    is_y32 = (brick_y == lane_s).astype(F32).astype(BF16)[:, 0:32]
    is_z2 = jnp.concatenate([is_z, is_z], axis=1)
    place, lane = iota((1024, 128), 0), iota((1024, 128), 1)
    for cy in range(4):
        gather[cy] = (lane == place // 128 * 16 + cy * 4 + place % 128 // 32).astype(F32).astype(BF16)
    slots[...] = sel[...].astype(BF16)

    for c in range(chunks):
        whole(1 + c, send2.at[c], recv2.at[c]).wait_recv()
        for k in range(per):
            part = recv2[c, :, k].astype(F32).reshape(256, 128).astype(BF16)
            by_x = dot(along_x, jnp.concatenate([part, part], axis=0))
            send3[c, :, k] = by_x.reshape(PEERS, 8, 128).astype(BF16)
        start(1 + chunks + c, mine, line_peer, line_shifts, send3.at[c], recv3.at[c])

    for c in range(chunks):
        whole(1 + chunks + c, send3.at[c], recv3.at[c]).wait_recv()
        for k in range(per):
            cy = c * per + k
            field[pl.ds(cy * 256, 256), :] = recv3[c, :, k].astype(F32).reshape(256, 128)
            taken = []
            for w in (0, 2, 4, 6):
                pair = [field[pl.ds(cy * 256 + w + u, 32, stride=8), :] for u in range(2)]
                rows = jnp.concatenate(pair, axis=1).astype(BF16)
                taken.append(jnp.where(is_z2, dot(is_y32, rows), 0.0).astype(BF16))
            gathered = dot(jnp.concatenate(taken, axis=1), gather[cy])
            if cy == 0:
                total[...] = gathered
            elif cy < 3:
                total[...] = total[...] + gathered
            else:
                send4[...] = (total[...] + gathered).astype(BF16).reshape(PEERS, 16, 128)
    last = 1 + 2 * chunks
    start(last, i, pts_peer, pts_shifts, send4, recv4)
    whole(0, send1, recv1).wait_send()
    for c in range(chunks):
        whole(1 + c, send2.at[c], recv2.at[c]).wait_send()
        whole(1 + chunks + c, send3.at[c], recv3.at[c]).wait_send()
    whole(last, send4, recv4).wait_recv()
    rows_ref[...] = dot(slots[...], recv4[...].reshape(PEERS * 16, 128))
    whole(last, send4, recv4).wait_send()


def points_kernel(usable_ref, rows_ref, weight_ref, cov_ref, adj_ref):
    lane8 = iota((8, 128), 1)
    left = lane8 < 64
    for b in range(0, weight_ref.shape[0], 2):
        first, second = rows_ref[pl.ds(b * 8, 8), :], rows_ref[pl.ds(b * 8 + 8, 8), :]
        four = jnp.concatenate(
            [
                jnp.where(left, first, 0.0), jnp.where(left, pltpu.roll(first, 64, 1), 0.0),
                jnp.where(left, 0.0, pltpu.roll(second, 64, 1)), jnp.where(left, 0.0, second),
            ],
            axis=0,
        )
        result = dot(four.astype(BF16), weight_ref[pl.ds(b, 2)].reshape(128, 128))
        for u in range(2):
            usable = usable_ref[b + u] > 0.0
            cov_ref[b + u] = jnp.where(usable, result[u * 16 : u * 16 + 8], 0.0)
            adj_ref[b + u] = jnp.where(usable, result[u * 16 + 8 : u * 16 + 16], 0.0)


CHUNKS = 4


def on_device(probes, weights, brick_owner, brick_slot, counts, length_scale):
    blocks = probes.shape[1]
    chunks = CHUNKS
    vmem = pl.BlockSpec(memory_space=pltpu.VMEM)
    small = pltpu.VMEM((PEERS, 16, 128), BF16)
    large = pltpu.VMEM((chunks, PEERS, 4 // chunks, 8, 128), BF16)
    rows, usable = pl.pallas_call(
        functools.partial(kernel, chunks),
        out_shape=(jax.ShapeDtypeStruct((blocks * 8, 128), F32), jax.ShapeDtypeStruct((blocks, 8, 128), F32)),
        in_specs=[pl.BlockSpec(memory_space=pl.ANY)] * 6,
        out_specs=(vmem, vmem),
        scratch_shapes=[
            pltpu.SMEM((1, blocks), I32),
            pltpu.SMEM((1, blocks), I32),
            pltpu.SMEM((1, blocks), I32),
            pltpu.SMEM((1, 1), F32),
            pltpu.VMEM(probes.shape[1:], BF16),
            pltpu.VMEM(weights.shape[1:], BF16),
            pltpu.VMEM((256, 128), F32),
            pltpu.VMEM((256, 512), F32),
            pltpu.VMEM((256, 512), BF16),
            pltpu.VMEM((512, 128), F32),
            pltpu.VMEM((512, 128), F32),
            pltpu.VMEM((1024, 128), F32),
            pltpu.VMEM((4, 1024, 128), BF16),
            pltpu.VMEM((512, 128), F32),
            small, small, large, large, large, large, small, small,
            pltpu.SemaphoreType.DMA((2 + 2 * chunks,)),
            pltpu.SemaphoreType.DMA((2 + 2 * chunks,)),
            pltpu.SemaphoreType.DMA((6,)),
            pltpu.SemaphoreType.REGULAR,
            pltpu.SemaphoreType.REGULAR,
        ],
        compiler_params=pltpu.CompilerParams(collective_id=0, has_side_effects=True, vmem_limit_bytes=24 << 20),
        name="covariance",
    )(
        *(
            pltpu.with_memory_space_constraint(a, pltpu.HBM)
            for a in (brick_owner.reshape(1, blocks), brick_slot, counts, probes[0], weights[0])
        ),
        length_scale,
    )
    out = jax.ShapeDtypeStruct((blocks, 8, 128), F32)
    cov, adj = pl.pallas_call(
        points_kernel,
        out_shape=(out, out),
        in_specs=[vmem, vmem, vmem],
        out_specs=(vmem, vmem),
        compiler_params=pltpu.CompilerParams(vmem_limit_bytes=16 << 20),
        name="points",
    )(usable, rows, weights[0])
    return cov[None], adj[None]


def solution(mesh):
    placed = (
        P("grid", "pts", None, None),
        P("grid", "pts", None, None),
        P("grid", "pts", None),
        P("grid", "pts"),
        P("grid", "pts"),
        P("grid", "pts"),
    )
    sharded = jax.shard_map(
        on_device,
        mesh=mesh,
        in_specs=placed,
        out_specs=(P("grid", "pts", None, None), P("grid", "pts", None, None)),
        check_vma=False,
    )

    def run(probes, weights, brick_owner, brick_slot, counts, length_scale):
        spread = jnp.broadcast_to(length_scale[None, :], brick_owner.shape[:1] + (mesh.shape["pts"],))
        return sharded(probes, weights, brick_owner, brick_slot, counts, spread)

    return run
```
